32 devices in a mesh: section: 4 (over y, x), dp: 8 (over z, core).
Axes of the slice: x: 2, y: 2, z: 4, core: 2. Of those that a mesh axis runs over, the one named last changes fastest.
Arguments:
- images: bfloat16 [4, 8, 8, 16, 768], P(None, 'dp'), may hold values from -6 to 6
- widths: int32 [4], replicated, may hold values from 0 to 2, as said below
- depth_kernel: bfloat16 [4, 7, 7, 768], P('section'), may hold values from -0.875 to 0.875
- depth_bias: bfloat16 [4, 768], P('section'), may hold values from -3 to 3
- ln_gain: bfloat16 [4, 768], P('section'), may hold values from 0.25 to 1.75
- ln_bias: bfloat16 [4, 768], P('section'), may hold values from -3 to 3
- w_in: bfloat16 [4, 1536, 768], P('section', 'dp'), may hold values from -0.21875 to 0.21875
- w_out: bfloat16 [4, 1536, 768], P('section', 'dp'), may hold values from -0.15625 to 0.15625
- layer_scale: bfloat16 [4, 768], P('section'), may hold values from 0.29882812 to 1
Outputs:
- section_acts: bfloat16 [4, 4, 8, 8, 16, 768], P('section', None, 'dp')
The draws below stay inside these ranges and needn't reach their ends.
Inputs may be any that keep to these rules, and one draw needn't show every extreme that they name: `widths`: each half of the micro-batches holds exactly one at level 0 and one at a level above 0; levels 1 and 2 both appear.
All inputs are finite; a program needn't handle non-finite values.
Results may differ from the reference program's by a relative error of at most 0.0065.
Values may be sent and summed in bfloat16 or wider, within the bound.
A program may use at most 64 MiB of HBM per device.

```python
import math
import jax
import jax.numpy as jnp
from jax import lax

C = 768
HID = 1536
KS = 7
MB = 4
HGT = 8
WID = 16
SECTIONS = 4
IMAGES = 8


def draw_widths(key, part):
    key_list = jax.random.split(key, 3)
    choose = jax.random.randint(key_list[0], (1,), 1, 3).astype(jnp.int32)
    zero_one = jnp.zeros((1,), jnp.int32)
    first_half = jax.random.permutation(key_list[1], jnp.concatenate([zero_one, choose]))
    second_half = jax.random.permutation(key_list[2], jnp.concatenate([zero_one, 3 - choose]))
    return jnp.concatenate([first_half, second_half]).astype(jnp.int32)


def levels(own_key, dims, cuts, least, largest):
    def one(axis_at, shards_of):
        heights = jax.random.uniform(jax.random.fold_in(jax.random.fold_in(own_key, 6), axis_at), (shards_of,), jnp.float32, least / len(cuts), largest / len(cuts))
        return jnp.repeat(jnp.exp(heights), dims[axis_at] // shards_of).reshape((-1,) + (1,) * (len(dims) - axis_at - 1))

    level = one(*cuts[0])
    for cut in cuts[1:]:
        level = level * one(*cut)
    return level


def noise(key, extent, spread, bound, cuts=(), kind=jnp.bfloat16):
    drawn = spread * jax.random.normal(key, extent, jnp.float32)
    if cuts:
        drawn = drawn * levels(key, extent, cuts, -0.22, 0.18)
    return jnp.clip(drawn, -bound, bound).astype(kind)


def setup_inputs(seed: int = 0) -> dict:
    key_of = jax.random.split(jax.random.key(seed), 10)
    images = noise(key_of[0], (MB, IMAGES, HGT, WID, C), 1.0, 6.0, ((1, 8),))
    widths = draw_widths(jax.random.fold_in(key_of[9], 71), 0)
    depth_kernel = noise(key_of[2], (SECTIONS, KS, KS, C), (KS * KS) ** -0.5, 0.875, ((0, 4),))
    depth_bias = noise(key_of[3], (SECTIONS, C), 0.5, 3.0, ((0, 4),))
    ln_gain = jnp.clip(1.0 + 0.15 * jax.random.normal(key_of[4], (SECTIONS, C), jnp.float32), 0.25, 1.75).astype(jnp.bfloat16)
    ln_bias = noise(key_of[5], (SECTIONS, C), 0.5, 3.0, ((0, 4),))
    w_in = noise(key_of[6], (SECTIONS, HID, C), C ** -0.5, 0.21875, ((0, 4), (1, 8)))
    w_out = noise(key_of[7], (SECTIONS, HID, C), HID ** -0.5, 0.15625, ((0, 4), (1, 8)))
    layer_scale = jnp.clip(jnp.exp(math.log(1.0) - 1.2078867 * jax.random.uniform(key_of[8], (SECTIONS, C), jnp.float32) ** levels(key_of[8], (SECTIONS, C), ((0, 4),), -0.2, 0.2)), 0.29882812, 1.0).astype(jnp.bfloat16)
    return dict(images=images, widths=widths, depth_kernel=depth_kernel, depth_bias=depth_bias, ln_gain=ln_gain, ln_bias=ln_bias, w_in=w_in, w_out=w_out, layer_scale=layer_scale)


def conv_block(inputs, width_level, depth_kernel, depth_bias, ln_gain, ln_bias, w_in, w_out, layer_scale):
    channels = inputs.shape[-1]
    hidden = w_in.shape[0]
    active_channels = jnp.where(width_level == 0, channels, jnp.where(width_level == 1, channels // 2, channels // 4))
    active_hidden = jnp.where(width_level == 0, hidden, jnp.where(width_level == 1, hidden // 2, hidden // 4))
    chan_mask = (jnp.arange(channels) < active_channels).astype(jnp.float32)
    hidden_mask = (jnp.arange(hidden) < active_hidden).astype(jnp.float32)
    channel_count = active_channels.astype(jnp.float32)
    widened = inputs.astype(jnp.float32) * chan_mask
    kernel = depth_kernel.astype(jnp.float32)
    reach = kernel.shape[0] // 2
    padded = jnp.pad(widened, ((0, 0), (reach, reach), (reach, reach), (0, 0)))
    rows_n = inputs.shape[1]
    cols_n = inputs.shape[2]
    spatial = jnp.zeros(widened.shape, jnp.float32)
    for row_off in range(kernel.shape[0]):
        for col_off in range(kernel.shape[1]):
            spatial = spatial + padded[:, row_off:row_off + rows_n, col_off:col_off + cols_n, :] * kernel[row_off, col_off]
    spatial = (spatial + depth_bias.astype(jnp.float32)) * chan_mask
    average = lax.optimization_barrier(jnp.sum(spatial, axis=-1, keepdims=True)) / channel_count
    centred = (spatial - average) * chan_mask
    variance = lax.optimization_barrier(jnp.sum(centred * centred, axis=-1, keepdims=True)) / channel_count
    normed = (centred * lax.rsqrt(variance + 1e-06) * ln_gain.astype(jnp.float32) + ln_bias.astype(jnp.float32)) * chan_mask
    flattened = normed.astype(jnp.bfloat16).reshape(-1, channels)
    expanded = jnp.dot(flattened, w_in.T, preferred_element_type=jnp.float32)
    activated = (jax.nn.gelu(expanded, approximate=True) * hidden_mask).astype(jnp.bfloat16)
    projected = jnp.dot(activated, w_out, preferred_element_type=jnp.float32).reshape(widened.shape)
    result = widened + layer_scale.astype(jnp.float32) * projected * chan_mask
    return result.astype(jnp.bfloat16)

def reference(images, widths, depth_kernel, depth_bias, ln_gain, ln_bias, w_in, w_out, layer_scale):
    collected = []
    for micro_index in range(MB):
        width_level = widths[micro_index]

        def section_step(carried, parameters):
            result = conv_block(carried, width_level, *parameters)
            return (result, result)
        _, stacked = lax.scan(section_step, images[micro_index], (depth_kernel, depth_bias, ln_gain, ln_bias, w_in, w_out, layer_scale))
        if micro_index >= MB // 2:
            stacked = stacked[::-1]
        collected.append(stacked)
    return jnp.stack(collected, axis=1)
```

```python
import functools

import jax
import jax.numpy as jnp
from jax import lax
from jax.experimental import pallas as pl
from jax.experimental.pallas import tpu as pltpu
from jax.sharding import PartitionSpec as P

MESH = pl.DeviceIdType.MESH
LANES = 128
LEFT = 8


def active_of(level, full):
    return jnp.where(level == 0, full, jnp.where(level == 1, full // 2, full // 4))


def relay_kernel(
    sections,
    shards,
    widths,
    images,
    depth_kernel,
    depth_bias,
    ln_gain,
    ln_bias,
    w_in,
    w_out,
    layer_scale,
    out,
    in_full,
    out_full,
    tiles,
    results,
    padded,
    spatial,
    normed,
    total,
    taps,
    local_sem,
    tile_sem,
    weight_send,
    weight_recv,
    tile_send,
    tile_recv,
    store_send,
    store_recv,
):
    position = lax.axis_index("section")
    rank = lax.axis_index("dp")
    chips = shards // 2
    chip = rank // 2
    core = rank % 2
    sibling = rank + 1 - 2 * core
    mirror = sections - 1 - position
    count, rows_n, cols_n, channels = tiles.shape
    halfway = count // 2
    hidden = in_full.shape[0]
    piece = hidden // shards
    side = depth_kernel.shape[1]
    reach = side // 2
    full = (in_full, out_full)

    def span(shard):
        return pl.ds(pl.multiple_of(shard * piece, 16), piece)

    own = [
        pltpu.make_async_copy(source.at[0], full[kind].at[span(rank)], local_sem.at[kind])
        for kind, source in enumerate((w_in, w_out))
    ]
    for copy in own:
        copy.start()

    def tile_in(slot):
        return pltpu.make_async_copy(images.at[slot, 0], tiles.at[slot], tile_sem.at[slot])

    @pl.when(position == 0)
    def _():
        for slot in range(count):
            tile_in(slot).start()

    barrier = pltpu.get_barrier_semaphore()
    pl.semaphore_signal(barrier, inc=1, device_id={"dp": sibling}, device_id_type=MESH)
    pl.semaphore_signal(barrier, inc=1, device_id={"section": mirror}, device_id_type=MESH)

    def greet(condition, target):
        @pl.when(condition)
        def _():
            pl.semaphore_signal(barrier, inc=1, device_id=target, device_id_type=MESH)

    greet(chip + 1 < chips, {"dp": rank + 2})
    greet(chip > 0, {"dp": rank - 2})
    greet(position + 1 < sections, {"section": position + 1})
    greet(position > 0, {"section": position - 1})

    for row in range(side):
        taps[row, 0:side, :] = depth_kernel[0, row].astype(jnp.float32)
    padded[:, 0:LEFT, :] = jnp.zeros((rows_n, LEFT, channels), jnp.float32)
    padded[:, LEFT + cols_n :, :] = jnp.zeros((rows_n, LEFT, channels), jnp.float32)
    for copy in own:
        copy.wait()

    greeted = 2 + sum(
        jnp.where(condition, 1, 0)
        for condition in (
            chip + 1 < chips,
            chip > 0,
            position + 1 < sections,
            position > 0,
        )
    )
    pl.semaphore_wait(barrier, greeted)

    @pl.when(position == 0)
    def _():
        for slot in range(count):
            tile_in(slot).wait()

    def weight_copy(kind, shard, target, lane, step):
        return pltpu.make_async_remote_copy(
            src_ref=full[kind].at[span(shard)],
            dst_ref=full[kind].at[span(shard)],
            send_sem=weight_send.at[kind, lane, step],
            recv_sem=weight_recv.at[kind, shard],
            device_id={"dp": target},
            device_id_type=MESH,
        )

    def conv_norm(slot):
        level = widths[slot]
        active = active_of(level, channels)
        mask_all = (lax.broadcasted_iota(jnp.int32, (1, channels), 1) < active).astype(jnp.float32)
        for row in range(rows_n):
            padded[row, LEFT : LEFT + cols_n, :] = (
                tiles[slot, row].astype(jnp.float32) * mask_all
            )

        def one_chunk(chunk, carried):
            start = pl.multiple_of(chunk * LANES, LANES)
            lanes = pl.ds(start, LANES)
            sums = [jnp.zeros((cols_n, LANES), jnp.float32) for _ in range(rows_n)]
            for col in range(side):
                rows = [
                    padded[row, pl.ds(LEFT - reach + col, cols_n), lanes] for row in range(rows_n)
                ]
                for row_off in range(side):
                    tap = taps[row_off, pl.ds(col, 1), lanes]
                    for row in range(rows_n):
                        source = row + row_off - reach
                        if 0 <= source < rows_n:
                            sums[row] = sums[row] + rows[source] * tap
            mask = (lax.broadcasted_iota(jnp.int32, (1, LANES), 1) + start < active).astype(
                jnp.float32
            )
            bias = depth_bias[:, lanes].astype(jnp.float32)
            for row in range(rows_n):
                spatial[row, :, lanes] = (sums[row] + bias) * mask
            return carried

        lax.fori_loop(0, channels // LANES, one_chunk, 0)
        inverse = 1.0 / jnp.full((1, 1), active, jnp.int32).astype(jnp.float32)
        gain = ln_gain[...].astype(jnp.float32)
        shift = ln_bias[...].astype(jnp.float32)

        def one_row(row, carried):
            value = spatial[row]
            average = jnp.sum(value, axis=-1, keepdims=True) * inverse
            centred = (value - average) * mask_all
            variance = jnp.sum(centred * centred, axis=-1, keepdims=True) * inverse
            result = (centred * lax.rsqrt(variance + 1e-06) * gain + shift) * mask_all
            normed[slot, pl.ds(pl.multiple_of(row * cols_n, 16), cols_n), :] = result.astype(
                jnp.bfloat16
            )
            return carried

        lax.fori_loop(0, rows_n, one_row, 0)

    def pointwise(slot):
        level = widths[slot]
        active = active_of(level, channels)
        active_hidden = active_of(level, hidden)
        width = 512 if hidden % 512 == 0 else hidden
        total[...] = jnp.zeros_like(total)

        def one_part(part, carried):
            start = pl.multiple_of(part * width, width)
            expanded = lax.dot_general(
                normed[slot],
                in_full[pl.ds(start, width), :],
                (((1,), (1,)), ((), ())),
                preferred_element_type=jnp.float32,
            )
            mask = (lax.broadcasted_iota(jnp.int32, (1, width), 1) + start < active_hidden).astype(
                jnp.float32
            )
            activated = (jax.nn.gelu(expanded, approximate=True) * mask).astype(jnp.bfloat16)
            total[...] += jnp.dot(
                activated, out_full[pl.ds(start, width), :], preferred_element_type=jnp.float32
            )
            return carried

        lax.fori_loop(0, hidden // width, one_part, 0)
        mask_all = (lax.broadcasted_iota(jnp.int32, (1, channels), 1) < active).astype(jnp.float32)
        scale = layer_scale[...].astype(jnp.float32) * mask_all
        for row in range(rows_n):
            value = tiles[slot, row].astype(jnp.float32) * mask_all
            value = value + scale * total[row * cols_n : (row + 1) * cols_n, :]
            results[slot, row] = value.astype(jnp.bfloat16)

    def gather_step(step, carried):
        rightward = chip - step
        leftward = chip + step
        for kind in range(2):
            @pl.when(rightward >= 0)
            def _():
                shard = 2 * rightward + core

                @pl.when(step > 0)
                def _():
                    weight_copy(kind, shard, sibling, 0, step).wait_recv()

                @pl.when(chip + 1 < chips)
                def _():
                    weight_copy(kind, shard, rank + 2, 0, step).start()

            @pl.when(leftward < chips)
            def _():
                shard = 2 * leftward + core

                @pl.when(step > 0)
                def _():
                    weight_copy(kind, shard, sibling, 1, step).wait_recv()

                @pl.when(chip > 0)
                def _():
                    weight_copy(kind, shard, rank - 2, 1, step).start()

                @pl.when(step > 0)
                def _():
                    weight_copy(kind, shard, sibling, 3, step).start()

            @pl.when(rightward >= 0)
            def _():
                weight_copy(kind, 2 * rightward + core, sibling, 2, step).start()

        @pl.when((position == 0) & (step < count))
        def _():
            conv_norm((step + halfway) % count)

        return carried

    lax.fori_loop(0, chips, gather_step, 0)

    def siblings_in(other, carried):
        for kind in range(2):
            weight_copy(kind, 2 * other + 1 - core, sibling, 0, 0).wait_recv()
        return carried

    lax.fori_loop(0, chips, siblings_in, 0)

    def forward(slot):
        return pltpu.make_async_remote_copy(
            src_ref=results.at[slot],
            dst_ref=tiles.at[slot],
            send_sem=tile_send.at[slot],
            recv_sem=tile_recv.at[slot],
            device_id={"section": position + 1},
            device_id_type=MESH,
        )

    def incoming(slot):
        return pltpu.make_async_remote_copy(
            src_ref=results.at[slot],
            dst_ref=tiles.at[slot],
            send_sem=tile_send.at[slot],
            recv_sem=tile_recv.at[slot],
            device_id={"section": mirror},
            device_id_type=MESH,
        )

    def across(slot):
        return pltpu.make_async_remote_copy(
            src_ref=results.at[slot],
            dst_ref=out.at[slot],
            send_sem=store_send.at[slot],
            recv_sem=store_recv.at[slot],
            device_id={"section": mirror},
            device_id_type=MESH,
        )

    def one_slot(index, carried):
        slot = (index + halfway) % count

        @pl.when(position > 0)
        def _():
            incoming(slot).wait_recv()

        @pl.when((position > 0) | (index >= chips))
        def _():
            conv_norm(slot)

        pointwise(slot)

        @pl.when(position + 1 < sections)
        def _():
            forward(slot).start()

        @pl.when(slot >= halfway)
        def _():
            across(slot).start()

        @pl.when(slot < halfway)
        def _():
            out[slot] = results[slot]

        return carried

    lax.fori_loop(0, count, one_slot, 0)

    def drain_weights(step, carried):
        for kind in range(2):
            @pl.when(chip - step >= 0)
            def _():
                shard = 2 * (chip - step) + core

                @pl.when(chip + 1 < chips)
                def _():
                    weight_copy(kind, shard, rank + 2, 0, step).wait_send()

                weight_copy(kind, shard, sibling, 2, step).wait_send()

            @pl.when(chip + step < chips)
            def _():
                shard = 2 * (chip + step) + core

                @pl.when(chip > 0)
                def _():
                    weight_copy(kind, shard, rank - 2, 1, step).wait_send()

                @pl.when(step > 0)
                def _():
                    weight_copy(kind, shard, sibling, 3, step).wait_send()

        return carried

    lax.fori_loop(0, chips, drain_weights, 0)

    for slot in range(count):
        @pl.when(position + 1 < sections)
        def _():
            forward(slot).wait_send()

        if slot >= halfway:
            across(slot).wait_send()
            across(slot).wait_recv()


def on_device(sections, shards, images, widths, *parameters):
    depth_kernel, depth_bias, ln_gain, ln_bias, w_in, w_out, layer_scale = parameters
    count, _, rows_n, cols_n, channels = images.shape
    side = depth_kernel.shape[1]
    hidden = w_in.shape[1] * shards
    tile = (count, rows_n, cols_n, channels)
    vmem = pl.BlockSpec(memory_space=pltpu.VMEM)
    anywhere = pl.BlockSpec(memory_space=pl.ANY)
    stored = pl.pallas_call(
        functools.partial(relay_kernel, sections, shards),
        out_shape=jax.ShapeDtypeStruct(tile, jnp.bfloat16),
        in_specs=[
            pl.BlockSpec(memory_space=pltpu.SMEM),
            anywhere,
            vmem,
            vmem,
            vmem,
            vmem,
            anywhere,
            anywhere,
            vmem,
        ],
        out_specs=vmem,
        scratch_shapes=[
            pltpu.VMEM((hidden, channels), jnp.bfloat16),
            pltpu.VMEM((hidden, channels), jnp.bfloat16),
            pltpu.VMEM(tile, jnp.bfloat16),
            pltpu.VMEM(tile, jnp.bfloat16),
            pltpu.VMEM((rows_n, cols_n + 2 * LEFT, channels), jnp.float32),
            pltpu.VMEM((rows_n, cols_n, channels), jnp.float32),
            pltpu.VMEM((count, rows_n * cols_n, channels), jnp.bfloat16),
            pltpu.VMEM((rows_n * cols_n, channels), jnp.float32),
            pltpu.VMEM((side, side + 1, channels), jnp.float32),
            pltpu.SemaphoreType.DMA((2,)),
            pltpu.SemaphoreType.DMA((count,)),
            pltpu.SemaphoreType.DMA((2, 4, shards // 2)),
            pltpu.SemaphoreType.DMA((2, shards)),
            pltpu.SemaphoreType.DMA((count,)),
            pltpu.SemaphoreType.DMA((count,)),
            pltpu.SemaphoreType.DMA((count,)),
            pltpu.SemaphoreType.DMA((count,)),
        ],
        compiler_params=pltpu.CompilerParams(collective_id=0, has_side_effects=True),
        name="relay",
    )(
        widths,
        images,
        depth_kernel,
        depth_bias,
        ln_gain,
        ln_bias,
        w_in,
        w_out,
        layer_scale,
    )
    return stored[None, :, None]


def solution(mesh):
    placed = (
        P(None, "dp", None, None, None),
        P(),
        P("section", None, None, None),
        P("section", None),
        P("section", None),
        P("section", None),
        P("section", "dp", None),
        P("section", "dp", None),
        P("section", None),
    )
    return jax.shard_map(
        functools.partial(on_device, mesh.shape["section"], mesh.shape["dp"]),
        mesh=mesh,
        in_specs=placed,
        out_specs=P("section", None, "dp", None, None, None),
        check_vma=False,
    )
```

```python
import functools

import jax
import jax.numpy as jnp
from jax import lax
from jax.experimental import pallas as pl
from jax.experimental.pallas import tpu as pltpu
from jax.sharding import PartitionSpec as P

MESH = pl.DeviceIdType.MESH
LANES = 128
LEFT = 8
PART = 256


def active_of(slot, full):
    return jnp.where(slot < 2, full, jnp.where(slot == 2, full // 2, full // 4))


def pieces_of(slot, full, width):
    return (active_of(slot, full) + width - 1) // width


def relay_kernel(
    sections,
    shards,
    widths,
    images,
    depth_kernel,
    depth_bias,
    ln_gain,
    ln_bias,
    w_in,
    w_out,
    layer_scale,
    out,
    in_full,
    out_full,
    tiles,
    results,
    staged,
    remote,
    padded,
    spatial,
    normed,
    total,
    activated,
    taps,
    local_sem,
    tile_sem,
    weight_send,
    weight_recv,
    tile_send,
    tile_recv,
    store_send,
    store_recv,
):
    position = lax.axis_index("section")
    rank = lax.axis_index("dp")
    chips = shards // 2
    chip = rank // 2
    core = rank % 2
    sibling = rank + 1 - 2 * core
    mirror = sections - 1 - position
    count, rows_n, cols_n, channels = tiles.shape
    hidden = in_full.shape[0]
    piece = hidden // shards
    side = depth_kernel.shape[1]
    reach = side // 2
    full = (in_full, out_full)

    def span(shard):
        return pl.ds(pl.multiple_of(shard * piece, 16), piece)

    own = [
        pltpu.make_async_copy(source.at[0], full[kind].at[span(rank)], local_sem.at[kind])
        for kind, source in enumerate((w_in, w_out))
    ]
    for copy in own:
        copy.start()

    full_low = jnp.where(widths[0] == 0, 0, 1)
    full_high = jnp.where(widths[2] == 0, 2, 3)
    half_low = jnp.where(widths[0] == 0, widths[1], widths[0]) == 1
    small_low = 1 - full_low
    small_high = 5 - full_high
    order = (
        full_high,
        full_low,
        jnp.where(half_low, small_low, small_high),
        jnp.where(half_low, small_high, small_low),
    )

    def tile_in(slot):
        return pltpu.make_async_copy(images.at[slot, 0], staged.at[slot], tile_sem.at[slot])

    @pl.when(position == 0)
    def _():
        for slot in range(count):
            tile_in(slot).start()

    for slot in range(1, count):
        for row in range(rows_n):
            results[slot, row] = jnp.zeros((cols_n, channels), jnp.bfloat16)
            remote[slot, row] = jnp.zeros((cols_n, channels), jnp.bfloat16)

    barrier = pltpu.get_barrier_semaphore()
    pl.semaphore_signal(barrier, inc=1, device_id={"dp": sibling}, device_id_type=MESH)
    pl.semaphore_signal(barrier, inc=1, device_id={"section": mirror}, device_id_type=MESH)

    def greet(condition, target):
        @pl.when(condition)
        def _():
            pl.semaphore_signal(barrier, inc=1, device_id=target, device_id_type=MESH)

    greet(chip + 1 < chips, {"dp": rank + 2})
    greet(chip > 0, {"dp": rank - 2})
    greet(position + 1 < sections, {"section": position + 1})
    greet(position > 0, {"section": position - 1})

    for row in range(side):
        taps[row, 0:side, :] = depth_kernel[0, row].astype(jnp.float32)
    padded[:, 0:LEFT, :] = jnp.zeros((rows_n, LEFT, channels), jnp.float32)
    padded[:, LEFT + cols_n :, :] = jnp.zeros((rows_n, LEFT, channels), jnp.float32)
    for copy in own:
        copy.wait()

    greeted = 2 + sum(
        jnp.where(condition, 1, 0)
        for condition in (
            chip + 1 < chips,
            chip > 0,
            position + 1 < sections,
            position > 0,
        )
    )
    pl.semaphore_wait(barrier, greeted)

    @pl.when(position == 0)
    def _():
        for slot in range(count):
            tile_in(slot).wait()
        for slot in range(count):
            tiles[slot] = staged[order[slot]]

    def weight_copy(kind, shard, target, lane, step):
        return pltpu.make_async_remote_copy(
            src_ref=full[kind].at[span(shard)],
            dst_ref=full[kind].at[span(shard)],
            send_sem=weight_send.at[kind, lane, step],
            recv_sem=weight_recv.at[kind, shard],
            device_id={"dp": target},
            device_id_type=MESH,
        )

    def conv_norm(slot):
        active = active_of(slot, channels)
        mask_all = (lax.broadcasted_iota(jnp.int32, (1, channels), 1) < active).astype(jnp.float32)

        def one_chunk(chunk, carried):
            start = pl.multiple_of(chunk * LANES, LANES)
            lanes = pl.ds(start, LANES)
            mask = (lax.broadcasted_iota(jnp.int32, (1, LANES), 1) + start < active).astype(
                jnp.float32
            )

            @pl.when((position > 0) & (chunk % (PART // LANES) == 0))
            def _():
                forward(slot, chunk // (PART // LANES), mirror).wait_recv()

            for row in range(rows_n):
                padded[row, LEFT : LEFT + cols_n, lanes] = (
                    tiles[slot, row, :, lanes].astype(jnp.float32) * mask
                )
            sums = [jnp.zeros((cols_n, LANES), jnp.float32) for _ in range(rows_n)]
            for col in range(side):
                rows = [
                    padded[row, pl.ds(LEFT - reach + col, cols_n), lanes] for row in range(rows_n)
                ]
                for row_off in range(side):
                    tap = taps[row_off, pl.ds(col, 1), lanes]
                    for row in range(rows_n):
                        source = row + row_off - reach
                        if 0 <= source < rows_n:
                            sums[row] = sums[row] + rows[source] * tap
            bias = depth_bias[:, lanes].astype(jnp.float32)
            for row in range(rows_n):
                spatial[row, :, lanes] = (sums[row] + bias) * mask
            return carried

        lax.fori_loop(
            0, pieces_of(slot, channels, PART) * (PART // LANES), one_chunk, 0
        )
        inverse = 1.0 / jnp.full((1, 1), active, jnp.int32).astype(jnp.float32)
        gain = ln_gain[...].astype(jnp.float32)
        shift = ln_bias[...].astype(jnp.float32)

        def one_row(row, carried):
            value = spatial[row] * mask_all
            average = jnp.sum(value, axis=-1, keepdims=True) * inverse
            centred = (value - average) * mask_all
            variance = jnp.sum(centred * centred, axis=-1, keepdims=True) * inverse
            result = (centred * lax.rsqrt(variance + 1e-06) * gain + shift) * mask_all
            normed[slot, pl.ds(pl.multiple_of(row * cols_n, 16), cols_n), :] = result.astype(
                jnp.bfloat16
            )
            return carried

        lax.fori_loop(0, rows_n, one_row, 0)

    def expand(slot, start, width):
        expanded = lax.dot_general(
            normed[slot],
            in_full[pl.ds(start, width), :],
            (((1,), (1,)), ((), ())),
            preferred_element_type=jnp.float32,
        )
        mask = (
            lax.broadcasted_iota(jnp.int32, (1, width), 1) + start < active_of(slot, hidden)
        ).astype(jnp.float32)
        return (jax.nn.gelu(expanded, approximate=True) * mask).astype(jnp.bfloat16)

    def add_chip(other):
        start = pl.multiple_of(other * 2 * piece, 2 * piece)

        def one_slot(slot, carried):
            @pl.when(start < active_of(slot, hidden))
            def _():
                total[slot] += jnp.dot(
                    expand(slot, start, 2 * piece),
                    out_full[pl.ds(start, 2 * piece), :],
                    preferred_element_type=jnp.float32,
                )

            return carried

        lax.fori_loop(0, count, one_slot, 0)

    width = 512 if hidden % 512 == 0 else hidden

    def activate(slot):
        def one_part(part, carried):
            start = pl.multiple_of(part * width, width)
            activated[:, pl.ds(start, width)] = expand(slot, start, width)
            return carried

        lax.fori_loop(0, pieces_of(slot, hidden, width), one_part, 0)

    def project(slot, part):
        lanes = pl.ds(pl.multiple_of(part * PART, PART), PART)

        def one_part(index, carried):
            start = pl.multiple_of(index * width, width)
            return carried + jnp.dot(
                activated[:, pl.ds(start, width)],
                out_full[pl.ds(start, width), lanes],
                preferred_element_type=jnp.float32,
            )

        total[slot, :, lanes] = lax.fori_loop(
            0,
            pieces_of(slot, hidden, width),
            one_part,
            jnp.zeros((rows_n * cols_n, PART), jnp.float32),
        )

    def finish(slot, part):
        start = pl.multiple_of(part * PART, PART)
        lanes = pl.ds(start, PART)
        mask = (
            lax.broadcasted_iota(jnp.int32, (1, PART), 1) + start < active_of(slot, channels)
        ).astype(jnp.float32)
        scale = layer_scale[:, lanes].astype(jnp.float32) * mask
        for row in range(rows_n):
            value = tiles[slot, row, :, lanes].astype(jnp.float32) * mask
            value = value + scale * total[slot, row * cols_n : (row + 1) * cols_n, lanes]
            results[slot, row, :, lanes] = value.astype(jnp.bfloat16)

    def forward(slot, part, target):
        lanes = pl.ds(pl.multiple_of(part * PART, PART), PART)
        return pltpu.make_async_remote_copy(
            src_ref=results.at[slot, :, :, lanes],
            dst_ref=tiles.at[slot, :, :, lanes],
            send_sem=tile_send.at[slot, part],
            recv_sem=tile_recv.at[slot, part],
            device_id={"section": target},
            device_id_type=MESH,
        )

    def across(slot, part):
        lanes = pl.ds(pl.multiple_of(part * PART, PART), PART)
        return pltpu.make_async_remote_copy(
            src_ref=results.at[slot, :, :, lanes],
            dst_ref=remote.at[slot, :, :, lanes],
            send_sem=store_send.at[slot, part],
            recv_sem=store_recv.at[slot, part],
            device_id={"section": mirror},
            device_id_type=MESH,
        )

    def each_part(slot, act):
        def one(part, carried):
            act(part)
            return carried

        lax.fori_loop(0, pieces_of(slot, channels, PART), one, 0)

    def norm_slot(slot, carried):
        total[slot] = jnp.zeros(total.shape[1:], jnp.float32)
        conv_norm(slot)
        return carried

    def gather_step(step, carried):
        rightward = chip - step
        leftward = chip + step
        for kind in range(2):
            @pl.when(rightward >= 0)
            def _():
                shard = 2 * rightward + core

                @pl.when(step > 0)
                def _():
                    weight_copy(kind, shard, sibling, 0, step).wait_recv()

                @pl.when(chip + 1 < chips)
                def _():
                    weight_copy(kind, shard, rank + 2, 0, step).start()

            @pl.when(leftward < chips)
            def _():
                shard = 2 * leftward + core

                @pl.when(step > 0)
                def _():
                    weight_copy(kind, shard, sibling, 1, step).wait_recv()

                @pl.when(chip > 0)
                def _():
                    weight_copy(kind, shard, rank - 2, 1, step).start()

                @pl.when(step > 0)
                def _():
                    weight_copy(kind, shard, sibling, 3, step).start()

            @pl.when(rightward >= 0)
            def _():
                weight_copy(kind, 2 * rightward + core, sibling, 2, step).start()

        def siblings_in(other):
            for kind in range(2):
                weight_copy(kind, 2 * other + 1 - core, sibling, 0, 0).wait_recv()

        @pl.when((position == 0) & (step == 0))
        def _():
            lax.fori_loop(0, count, norm_slot, 0)

        @pl.when(rightward >= 0)
        def _():
            siblings_in(rightward)

            @pl.when(position == 0)
            def _():
                add_chip(rightward)

        @pl.when((leftward < chips) & (step > 0))
        def _():
            siblings_in(leftward)

            @pl.when(position == 0)
            def _():
                add_chip(leftward)

        return carried

    lax.fori_loop(0, chips, gather_step, 0)

    def one_slot(slot, carried):
        @pl.when(position > 0)
        def _():
            conv_norm(slot)
            activate(slot)

        def one_part(part):
            @pl.when(position > 0)
            def _():
                project(slot, part)

            finish(slot, part)

            @pl.when(position + 1 < sections)
            def _():
                forward(slot, part, position + 1).start()

        each_part(slot, one_part)

        @pl.when(slot != 1)
        def _():
            each_part(slot, lambda part: across(slot, part).start())

        return carried

    lax.fori_loop(0, count, one_slot, 0)

    def drain_weights(step, carried):
        for kind in range(2):
            @pl.when(chip - step >= 0)
            def _():
                shard = 2 * (chip - step) + core

                @pl.when(chip + 1 < chips)
                def _():
                    weight_copy(kind, shard, rank + 2, 0, step).wait_send()

                weight_copy(kind, shard, sibling, 2, step).wait_send()

            @pl.when(chip + step < chips)
            def _():
                shard = 2 * (chip + step) + core

                @pl.when(chip > 0)
                def _():
                    weight_copy(kind, shard, rank - 2, 1, step).wait_send()

                @pl.when(step > 0)
                def _():
                    weight_copy(kind, shard, sibling, 3, step).wait_send()

        return carried

    lax.fori_loop(0, chips, drain_weights, 0)

    out[0] = results[jnp.where(full_low == 0, 1, jnp.where(half_low, 2, 3))]
    out[1] = results[jnp.where(full_low == 1, 1, jnp.where(half_low, 2, 3))]

    def drain_slot(slot, carried):
        @pl.when(position + 1 < sections)
        def _():
            each_part(slot, lambda part: forward(slot, part, mirror).wait_send())

        @pl.when(slot != 1)
        def _():
            each_part(slot, lambda part: across(slot, part).wait_send())
            each_part(slot, lambda part: across(slot, part).wait_recv())

        return carried

    lax.fori_loop(0, count, drain_slot, 0)
    out[2] = remote[jnp.where(full_high == 2, 0, jnp.where(half_low, 3, 2))]
    out[3] = remote[jnp.where(full_high == 3, 0, jnp.where(half_low, 3, 2))]


def on_device(sections, shards, images, widths, *parameters):
    depth_kernel, depth_bias, ln_gain, ln_bias, w_in, w_out, layer_scale = parameters
    count, _, rows_n, cols_n, channels = images.shape
    side = depth_kernel.shape[1]
    hidden = w_in.shape[1] * shards
    tile = (count, rows_n, cols_n, channels)
    vmem = pl.BlockSpec(memory_space=pltpu.VMEM)
    anywhere = pl.BlockSpec(memory_space=pl.ANY)
    stored = pl.pallas_call(
        functools.partial(relay_kernel, sections, shards),
        out_shape=jax.ShapeDtypeStruct(tile, jnp.bfloat16),
        in_specs=[
            pl.BlockSpec(memory_space=pltpu.SMEM),
            anywhere,
            vmem,
            vmem,
            vmem,
            vmem,
            anywhere,
            anywhere,
            vmem,
        ],
        out_specs=vmem,
        scratch_shapes=[
            pltpu.VMEM((hidden, channels), jnp.bfloat16),
            pltpu.VMEM((hidden, channels), jnp.bfloat16),
            pltpu.VMEM(tile, jnp.bfloat16),
            pltpu.VMEM(tile, jnp.bfloat16),
            pltpu.VMEM(tile, jnp.bfloat16),
            pltpu.VMEM(tile, jnp.bfloat16),
            pltpu.VMEM((rows_n, cols_n + 2 * LEFT, channels), jnp.float32),
            pltpu.VMEM((rows_n, cols_n, channels), jnp.float32),
            pltpu.VMEM((count, rows_n * cols_n, channels), jnp.bfloat16),
            pltpu.VMEM((count, rows_n * cols_n, channels), jnp.float32),
            pltpu.VMEM((rows_n * cols_n, hidden), jnp.bfloat16),
            pltpu.VMEM((side, side + 1, channels), jnp.float32),
            pltpu.SemaphoreType.DMA((2,)),
            pltpu.SemaphoreType.DMA((count,)),
            pltpu.SemaphoreType.DMA((2, 4, shards // 2)),
            pltpu.SemaphoreType.DMA((2, shards)),
            pltpu.SemaphoreType.DMA((count, channels // PART)),
            pltpu.SemaphoreType.DMA((count, channels // PART)),
            pltpu.SemaphoreType.DMA((count, channels // PART)),
            pltpu.SemaphoreType.DMA((count, channels // PART)),
        ],
        compiler_params=pltpu.CompilerParams(collective_id=0, has_side_effects=True),
        name="relay",
    )(
        widths,
        images,
        depth_kernel,
        depth_bias,
        ln_gain,
        ln_bias,
        w_in,
        w_out,
        layer_scale,
    )
    return stored[None, :, None]


def solution(mesh):
    placed = (
        P(None, "dp", None, None, None),
        P(),
        P("section", None, None, None),
        P("section", None),
        P("section", None),
        P("section", None),
        P("section", "dp", None),
        P("section", "dp", None),
        P("section", None),
    )
    return jax.shard_map(
        functools.partial(on_device, mesh.shape["section"], mesh.shape["dp"]),
        mesh=mesh,
        in_specs=placed,
        out_specs=P("section", None, "dp", None, None, None),
        check_vma=False,
    )
```

```python
import functools

import jax
import jax.numpy as jnp
from jax import lax
from jax.experimental import pallas as pl
from jax.experimental.pallas import tpu as pltpu
from jax.sharding import PartitionSpec as P

MESH = pl.DeviceIdType.MESH
LANES = 128
LEFT = 8
PART = 256


def active_of(slot, full):
    return jnp.where(slot < 2, full, jnp.where(slot == 2, full // 2, full // 4))


def pieces_of(slot, full, width):
    return (active_of(slot, full) + width - 1) // width


def relay_kernel(
    sections,
    shards,
    widths,
    images,
    depth_kernel,
    depth_bias,
    ln_gain,
    ln_bias,
    w_in,
    w_out,
    layer_scale,
    out,
    in_full,
    out_full,
    tiles,
    results,
    staged,
    remote,
    padded,
    spatial,
    normed,
    total,
    activated,
    taps,
    local_sem,
    tile_sem,
    weight_send,
    weight_recv,
    tile_send,
    tile_recv,
    store_send,
    store_recv,
):
    position = lax.axis_index("section")
    rank = lax.axis_index("dp")
    chips = shards // 2
    chip = rank // 2
    core = rank % 2
    sibling = rank + 1 - 2 * core
    mirror = sections - 1 - position
    count, rows_n, cols_n, channels = tiles.shape
    hidden = in_full.shape[0]
    piece = hidden // shards
    side = depth_kernel.shape[1]
    reach = side // 2
    full = (in_full, out_full)

    def span(shard):
        return pl.ds(pl.multiple_of(shard * piece, 16), piece)

    own = [
        pltpu.make_async_copy(source.at[0], full[kind].at[span(rank)], local_sem.at[kind])
        for kind, source in enumerate((w_in, w_out))
    ]
    for copy in own:
        copy.start()

    full_low = jnp.where(widths[0] == 0, 0, 1)
    full_high = jnp.where(widths[2] == 0, 2, 3)
    half_low = jnp.where(widths[0] == 0, widths[1], widths[0]) == 1
    small_low = 1 - full_low
    small_high = 5 - full_high
    order = (
        full_high,
        full_low,
        jnp.where(half_low, small_low, small_high),
        jnp.where(half_low, small_high, small_low),
    )

    def tile_in(slot):
        return pltpu.make_async_copy(images.at[slot, 0], staged.at[slot], tile_sem.at[slot])

    @pl.when(position == 0)
    def _():
        for slot in range(count):
            tile_in(slot).start()

    for slot in range(1, count):
        for row in range(rows_n):
            results[slot, row] = jnp.zeros((cols_n, channels), jnp.bfloat16)
            remote[slot, row] = jnp.zeros((cols_n, channels), jnp.bfloat16)

    barrier = pltpu.get_barrier_semaphore()
    pl.semaphore_signal(barrier, inc=1, device_id={"dp": sibling}, device_id_type=MESH)
    pl.semaphore_signal(barrier, inc=1, device_id={"section": mirror}, device_id_type=MESH)

    def greet(condition, target):
        @pl.when(condition)
        def _():
            pl.semaphore_signal(barrier, inc=1, device_id=target, device_id_type=MESH)

    greet(chip + 1 < chips, {"dp": rank + 2})
    greet(chip > 0, {"dp": rank - 2})
    greet(position + 1 < sections, {"section": position + 1})
    greet(position > 0, {"section": position - 1})

    for row in range(side):
        taps[row, 0:side, :] = depth_kernel[0, row].astype(jnp.float32)
    padded[:, 0:LEFT, :] = jnp.zeros((rows_n, LEFT, channels), jnp.float32)
    padded[:, LEFT + cols_n :, :] = jnp.zeros((rows_n, LEFT, channels), jnp.float32)
    for copy in own:
        copy.wait()

    greeted = 2 + sum(
        jnp.where(condition, 1, 0)
        for condition in (
            chip + 1 < chips,
            chip > 0,
            position + 1 < sections,
            position > 0,
        )
    )
    pl.semaphore_wait(barrier, greeted)

    @pl.when(position == 0)
    def _():
        for slot in range(count):
            tile_in(slot).wait()
        for slot in range(count):
            tiles[slot] = staged[order[slot]]

    def weight_copy(kind, shard, target, lane, step):
        return pltpu.make_async_remote_copy(
            src_ref=full[kind].at[span(shard)],
            dst_ref=full[kind].at[span(shard)],
            send_sem=weight_send.at[kind, lane, step],
            recv_sem=weight_recv.at[kind, shard],
            device_id={"dp": target},
            device_id_type=MESH,
        )

    def conv_norm(slot):
        active = active_of(slot, channels)
        mask_all = (lax.broadcasted_iota(jnp.int32, (1, channels), 1) < active).astype(jnp.float32)

        def one_chunk(chunk, carried):
            start = pl.multiple_of(chunk * LANES, LANES)
            lanes = pl.ds(start, LANES)
            mask = (lax.broadcasted_iota(jnp.int32, (1, LANES), 1) + start < active).astype(
                jnp.float32
            )

            @pl.when((position > 0) & (chunk % (PART // LANES) == 0))
            def _():
                forward(slot, chunk // (PART // LANES), mirror).wait_recv()

            for row in range(rows_n):
                padded[row, LEFT : LEFT + cols_n, lanes] = (
                    tiles[slot, row, :, lanes].astype(jnp.float32) * mask
                )
            sums = [jnp.zeros((cols_n, LANES), jnp.float32) for _ in range(rows_n)]
            for col in range(side):
                rows = [
                    padded[row, pl.ds(LEFT - reach + col, cols_n), lanes] for row in range(rows_n)
                ]
                for row_off in range(side):
                    tap = taps[row_off, pl.ds(col, 1), lanes]
                    for row in range(rows_n):
                        source = row + row_off - reach
                        if 0 <= source < rows_n:
                            sums[row] = sums[row] + rows[source] * tap
            bias = depth_bias[:, lanes].astype(jnp.float32)
            for row in range(rows_n):
                spatial[row, :, lanes] = (sums[row] + bias) * mask
            return carried

        lax.fori_loop(
            0, pieces_of(slot, channels, PART) * (PART // LANES), one_chunk, 0
        )
        inverse = 1.0 / jnp.full((1, 1), active, jnp.int32).astype(jnp.float32)
        gain = ln_gain[...].astype(jnp.float32)
        shift = ln_bias[...].astype(jnp.float32)

        def one_row(row, carried):
            value = spatial[row] * mask_all
            average = jnp.sum(value, axis=-1, keepdims=True) * inverse
            centred = (value - average) * mask_all
            variance = jnp.sum(centred * centred, axis=-1, keepdims=True) * inverse
            result = (centred * lax.rsqrt(variance + 1e-06) * gain + shift) * mask_all
            normed[slot, pl.ds(pl.multiple_of(row * cols_n, 16), cols_n), :] = result.astype(
                jnp.bfloat16
            )
            return carried

        lax.fori_loop(0, rows_n, one_row, 0)

    def expand(slot, start, width):
        expanded = lax.dot_general(
            normed[slot],
            in_full[pl.ds(start, width), :],
            (((1,), (1,)), ((), ())),
            preferred_element_type=jnp.float32,
        )
        mask = (
            lax.broadcasted_iota(jnp.int32, (1, width), 1) + start < active_of(slot, hidden)
        ).astype(jnp.float32)
        return (jax.nn.gelu(expanded, approximate=True) * mask).astype(jnp.bfloat16)

    def add_to(slot, start):
        @pl.when(start < active_of(slot, hidden))
        def _():
            total[slot] += jnp.dot(
                expand(slot, start, 2 * piece),
                out_full[pl.ds(start, 2 * piece), :],
                preferred_element_type=jnp.float32,
            )

    def add_chip(other):
        start = pl.multiple_of(other * 2 * piece, 2 * piece)

        def one_slot(slot, carried):
            add_to(slot, start)
            return carried

        lax.fori_loop(0, count, one_slot, 0)

    width = 512 if hidden % 512 == 0 else hidden

    def activate(slot):
        def one_part(part, carried):
            start = pl.multiple_of(part * width, width)
            activated[:, pl.ds(start, width)] = expand(slot, start, width)
            return carried

        lax.fori_loop(0, pieces_of(slot, hidden, width), one_part, 0)

    def project(slot, part):
        lanes = pl.ds(pl.multiple_of(part * PART, PART), PART)

        def one_part(index, carried):
            start = pl.multiple_of(index * width, width)
            return carried + jnp.dot(
                activated[:, pl.ds(start, width)],
                out_full[pl.ds(start, width), lanes],
                preferred_element_type=jnp.float32,
            )

        total[slot, :, lanes] = lax.fori_loop(
            0,
            pieces_of(slot, hidden, width),
            one_part,
            jnp.zeros((rows_n * cols_n, PART), jnp.float32),
        )

    def finish(slot, part):
        start = pl.multiple_of(part * PART, PART)
        lanes = pl.ds(start, PART)
        mask = (
            lax.broadcasted_iota(jnp.int32, (1, PART), 1) + start < active_of(slot, channels)
        ).astype(jnp.float32)
        scale = layer_scale[:, lanes].astype(jnp.float32) * mask
        for row in range(rows_n):
            value = tiles[slot, row, :, lanes].astype(jnp.float32) * mask
            value = value + scale * total[slot, row * cols_n : (row + 1) * cols_n, lanes]
            results[slot, row, :, lanes] = value.astype(jnp.bfloat16)

    def forward(slot, part, target):
        lanes = pl.ds(pl.multiple_of(part * PART, PART), PART)
        return pltpu.make_async_remote_copy(
            src_ref=results.at[slot, :, :, lanes],
            dst_ref=tiles.at[slot, :, :, lanes],
            send_sem=tile_send.at[slot, part],
            recv_sem=tile_recv.at[slot, part],
            device_id={"section": target},
            device_id_type=MESH,
        )

    def across(slot, part):
        lanes = pl.ds(pl.multiple_of(part * PART, PART), PART)
        return pltpu.make_async_remote_copy(
            src_ref=results.at[slot, :, :, lanes],
            dst_ref=remote.at[slot, :, :, lanes],
            send_sem=store_send.at[slot, part],
            recv_sem=store_recv.at[slot, part],
            device_id={"section": mirror},
            device_id_type=MESH,
        )

    def each_part(slot, act):
        def one(part, carried):
            act(part)
            return carried

        lax.fori_loop(0, pieces_of(slot, channels, PART), one, 0)

    def norm_slot(slot, carried):
        total[slot] = jnp.zeros(total.shape[1:], jnp.float32)
        conv_norm(slot)
        return carried

    def siblings_in(other):
        for kind in range(2):
            weight_copy(kind, 2 * other + 1 - core, sibling, 0, 0).wait_recv()

    def absorb(step):
        rightward = chip - step
        leftward = chip + step

        @pl.when(rightward >= 0)
        def _():
            siblings_in(rightward)

            @pl.when(position == 0)
            def _():
                add_chip(rightward)

        @pl.when((leftward < chips) & (step > 0))
        def _():
            siblings_in(leftward)

            @pl.when(position == 0)
            def _():
                add_chip(leftward)

    def gather_step(step, carried):
        rightward = chip - step
        leftward = chip + step

        @pl.when((position == 0) & (step == 1))
        def _():
            lax.fori_loop(2, count, norm_slot, 0)

        @pl.when(step > 0)
        def _():
            absorb(step - 1)

        for kind in range(2):
            @pl.when(rightward >= 0)
            def _():
                shard = 2 * rightward + core

                @pl.when(step > 0)
                def _():
                    weight_copy(kind, shard, sibling, 0, step).wait_recv()

                @pl.when(chip + 1 < chips)
                def _():
                    weight_copy(kind, shard, rank + 2, 0, step).start()

            @pl.when(leftward < chips)
            def _():
                shard = 2 * leftward + core

                @pl.when(step > 0)
                def _():
                    weight_copy(kind, shard, sibling, 1, step).wait_recv()

                @pl.when(chip > 0)
                def _():
                    weight_copy(kind, shard, rank - 2, 1, step).start()

                @pl.when(step > 0)
                def _():
                    weight_copy(kind, shard, sibling, 3, step).start()

            @pl.when(rightward >= 0)
            def _():
                weight_copy(kind, 2 * rightward + core, sibling, 2, step).start()

        @pl.when((position == 0) & (step == 0))
        def _():
            lax.fori_loop(0, 2, norm_slot, 0)

        return carried

    lax.fori_loop(0, chips, gather_step, 0)
    at_end = (chip == 0) | (chip == chips - 1)
    far = chips - 1 - chip
    far_start = pl.multiple_of(far * 2 * piece, 2 * piece)

    @pl.when(at_end)
    def _():
        siblings_in(far)

    def one_slot(slot, carried):
        @pl.when(position > 0)
        def _():
            conv_norm(slot)
            activate(slot)

        @pl.when((position == 0) & at_end)
        def _():
            add_to(slot, far_start)

        def one_part(part):
            @pl.when(position > 0)
            def _():
                project(slot, part)

            finish(slot, part)

            @pl.when(position + 1 < sections)
            def _():
                forward(slot, part, position + 1).start()

        each_part(slot, one_part)

        @pl.when((slot != 1) & (position == sections - 1))
        def _():
            each_part(slot, lambda part: across(slot, part).start())

        return carried

    lax.fori_loop(0, count, one_slot, 0)
    sends_across = position != sections // 2 - 1
    takes_across = position != sections // 2

    def store_slot(slot, carried):
        @pl.when((slot != 1) & (position < sections - 1) & sends_across)
        def _():
            each_part(slot, lambda part: across(slot, part).start())

        def keep(part):
            lanes = pl.ds(pl.multiple_of(part * PART, PART), PART)
            for row in range(rows_n):
                remote[slot, row, :, lanes] = tiles[slot, row, :, lanes]

        @pl.when((slot != 1) & (position == sections // 2))
        def _():
            each_part(slot, keep)

        return carried

    lax.fori_loop(0, count, store_slot, 0)

    def drain_weights(step, carried):
        for kind in range(2):
            @pl.when(chip - step >= 0)
            def _():
                shard = 2 * (chip - step) + core

                @pl.when(chip + 1 < chips)
                def _():
                    weight_copy(kind, shard, rank + 2, 0, step).wait_send()

                weight_copy(kind, shard, sibling, 2, step).wait_send()

            @pl.when(chip + step < chips)
            def _():
                shard = 2 * (chip + step) + core

                @pl.when(chip > 0)
                def _():
                    weight_copy(kind, shard, rank - 2, 1, step).wait_send()

                @pl.when(step > 0)
                def _():
                    weight_copy(kind, shard, sibling, 3, step).wait_send()

        return carried

    lax.fori_loop(0, chips, drain_weights, 0)

    out[0] = results[jnp.where(full_low == 0, 1, jnp.where(half_low, 2, 3))]
    out[1] = results[jnp.where(full_low == 1, 1, jnp.where(half_low, 2, 3))]

    def drain_slot(slot, carried):
        @pl.when(position + 1 < sections)
        def _():
            each_part(slot, lambda part: forward(slot, part, mirror).wait_send())

        @pl.when((slot != 1) & sends_across)
        def _():
            each_part(slot, lambda part: across(slot, part).wait_send())

        @pl.when((slot != 1) & takes_across)
        def _():
            each_part(slot, lambda part: across(slot, part).wait_recv())

        return carried

    lax.fori_loop(0, count, drain_slot, 0)
    out[2] = remote[jnp.where(full_high == 2, 0, jnp.where(half_low, 3, 2))]
    out[3] = remote[jnp.where(full_high == 3, 0, jnp.where(half_low, 3, 2))]


def on_device(sections, shards, images, widths, *parameters):
    depth_kernel, depth_bias, ln_gain, ln_bias, w_in, w_out, layer_scale = parameters
    count, _, rows_n, cols_n, channels = images.shape
    side = depth_kernel.shape[1]
    hidden = w_in.shape[1] * shards
    tile = (count, rows_n, cols_n, channels)
    vmem = pl.BlockSpec(memory_space=pltpu.VMEM)
    anywhere = pl.BlockSpec(memory_space=pl.ANY)
    stored = pl.pallas_call(
        functools.partial(relay_kernel, sections, shards),
        out_shape=jax.ShapeDtypeStruct(tile, jnp.bfloat16),
        in_specs=[
            pl.BlockSpec(memory_space=pltpu.SMEM),
            anywhere,
            vmem,
            vmem,
            vmem,
            vmem,
            anywhere,
            anywhere,
            vmem,
        ],
        out_specs=vmem,
        scratch_shapes=[
            pltpu.VMEM((hidden, channels), jnp.bfloat16),
            pltpu.VMEM((hidden, channels), jnp.bfloat16),
            pltpu.VMEM(tile, jnp.bfloat16),
            pltpu.VMEM(tile, jnp.bfloat16),
            pltpu.VMEM(tile, jnp.bfloat16),
            pltpu.VMEM(tile, jnp.bfloat16),
            pltpu.VMEM((rows_n, cols_n + 2 * LEFT, channels), jnp.float32),
            pltpu.VMEM((rows_n, cols_n, channels), jnp.float32),
            pltpu.VMEM((count, rows_n * cols_n, channels), jnp.bfloat16),
            pltpu.VMEM((count, rows_n * cols_n, channels), jnp.float32),
            pltpu.VMEM((rows_n * cols_n, hidden), jnp.bfloat16),
            pltpu.VMEM((side, side + 1, channels), jnp.float32),
            pltpu.SemaphoreType.DMA((2,)),
            pltpu.SemaphoreType.DMA((count,)),
            pltpu.SemaphoreType.DMA((2, 4, shards // 2)),
            pltpu.SemaphoreType.DMA((2, shards)),
            pltpu.SemaphoreType.DMA((count, channels // PART)),
            pltpu.SemaphoreType.DMA((count, channels // PART)),
            pltpu.SemaphoreType.DMA((count, channels // PART)),
            pltpu.SemaphoreType.DMA((count, channels // PART)),
        ],
        compiler_params=pltpu.CompilerParams(collective_id=0, has_side_effects=True),
        name="relay",
    )(
        widths,
        images,
        depth_kernel,
        depth_bias,
        ln_gain,
        ln_bias,
        w_in,
        w_out,
        layer_scale,
    )
    return stored[None, :, None]


def solution(mesh):
    placed = (
        P(None, "dp", None, None, None),
        P(),
        P("section", None, None, None),
        P("section", None),
        P("section", None),
        P("section", None),
        P("section", "dp", None),
        P("section", "dp", None),
        P("section", None),
    )
    return jax.shard_map(
        functools.partial(on_device, mesh.shape["section"], mesh.shape["dp"]),
        mesh=mesh,
        in_specs=placed,
        out_specs=P("section", None, "dp", None, None, None),
        check_vma=False,
    )
```

```python
import functools

import jax
import jax.numpy as jnp
from jax import lax
from jax.experimental import pallas as pl
from jax.experimental.pallas import tpu as pltpu
from jax.sharding import PartitionSpec as P

MESH = pl.DeviceIdType.MESH
LANES = 128
LEFT = 8
PART = 256
SUB = 8


def active_of(slot, full):
    return jnp.where(slot < 2, full, jnp.where(slot == 2, full // 2, full // 4))


def pieces_of(slot, full, width):
    return (active_of(slot, full) + width - 1) // width


def relay_kernel(
    sections,
    shards,
    widths,
    images,
    depth_kernel,
    depth_bias,
    ln_gain,
    ln_bias,
    w_in,
    w_out,
    layer_scale,
    out,
    in_full,
    out_full,
    tiles,
    results,
    staged,
    remote,
    padded,
    spatial,
    normed,
    total,
    activated,
    taps,
    local_sem,
    tile_sem,
    weight_send,
    weight_recv,
    tile_send,
    tile_recv,
    store_send,
    store_recv,
):
    position = lax.axis_index("section")
    rank = lax.axis_index("dp")
    chips = shards // 2
    chip = rank // 2
    core = rank % 2
    sibling = rank + 1 - 2 * core
    mirror = sections - 1 - position
    count, rows_n, cols_n, channels = tiles.shape
    hidden = in_full.shape[0]
    piece = hidden // shards
    side = depth_kernel.shape[1]
    reach = side // 2
    full = (in_full, out_full)

    def span(shard):
        return pl.ds(pl.multiple_of(shard * piece, 16), piece)

    own = [
        pltpu.make_async_copy(source.at[0], full[kind].at[span(rank)], local_sem.at[kind])
        for kind, source in enumerate((w_in, w_out))
    ]
    for copy in own:
        copy.start()

    full_low = jnp.where(widths[0] == 0, 0, 1)
    full_high = jnp.where(widths[2] == 0, 2, 3)
    half_low = jnp.where(widths[0] == 0, widths[1], widths[0]) == 1
    small_low = 1 - full_low
    small_high = 5 - full_high
    order = (
        full_high,
        full_low,
        jnp.where(half_low, small_low, small_high),
        jnp.where(half_low, small_high, small_low),
    )

    def tile_in(slot):
        return pltpu.make_async_copy(images.at[slot, 0], staged.at[slot], tile_sem.at[slot])

    @pl.when(position == 0)
    def _():
        for slot in range(count):
            tile_in(slot).start()

    for slot in range(1, count):
        for row in range(rows_n):
            results[slot, row] = jnp.zeros((cols_n, channels), jnp.bfloat16)
            remote[slot, row] = jnp.zeros((cols_n, channels), jnp.bfloat16)

    barrier = pltpu.get_barrier_semaphore()
    pl.semaphore_signal(barrier, inc=1, device_id={"dp": sibling}, device_id_type=MESH)
    pl.semaphore_signal(barrier, inc=1, device_id={"section": mirror}, device_id_type=MESH)

    def greet(condition, target):
        @pl.when(condition)
        def _():
            pl.semaphore_signal(barrier, inc=1, device_id=target, device_id_type=MESH)

    greet(chip + 1 < chips, {"dp": rank + 2})
    greet(chip > 0, {"dp": rank - 2})
    greet(position + 1 < sections, {"section": position + 1})
    greet(position > 0, {"section": position - 1})

    for row in range(rows_n):
        padded[row, 0:LEFT, :] = jnp.zeros((LEFT, LANES), jnp.float32)
        padded[row, LEFT + cols_n :, :] = jnp.zeros((LEFT, LANES), jnp.float32)

    def spread(chunk, carried):
        lanes = pl.ds(pl.multiple_of(chunk * LANES, LANES), LANES)
        for row in range(side):
            strip = depth_kernel[0, row, :, lanes].astype(jnp.float32)
            for col in range(side):
                taps[chunk, row * side + col] = jnp.broadcast_to(
                    strip[col : col + 1, :], (SUB, LANES)
                )
        return carried

    lax.fori_loop(0, channels // LANES, spread, 0)
    for copy in own:
        copy.wait()

    greeted = 2 + sum(
        jnp.where(condition, 1, 0)
        for condition in (
            chip + 1 < chips,
            chip > 0,
            position + 1 < sections,
            position > 0,
        )
    )
    pl.semaphore_wait(barrier, greeted)

    @pl.when(position == 0)
    def _():
        for slot in range(count):
            tile_in(slot).wait()
        for slot in range(count):
            tiles[slot] = staged[order[slot]]

    def weight_copy(kind, shard, target, lane, step):
        return pltpu.make_async_remote_copy(
            src_ref=full[kind].at[span(shard)],
            dst_ref=full[kind].at[span(shard)],
            send_sem=weight_send.at[kind, lane, step],
            recv_sem=weight_recv.at[kind, shard],
            device_id={"dp": target},
            device_id_type=MESH,
        )

    def conv_norm(slot):
        active = active_of(slot, channels)
        mask_all = (lax.broadcasted_iota(jnp.int32, (1, channels), 1) < active).astype(jnp.float32)

        def one_chunk(chunk, carried):
            start = pl.multiple_of(chunk * LANES, LANES)
            lanes = pl.ds(start, LANES)
            mask = (lax.broadcasted_iota(jnp.int32, (1, LANES), 1) + start < active).astype(
                jnp.float32
            )

            @pl.when((position > 0) & (chunk % (PART // LANES) == 0))
            def _():
                forward(slot, chunk // (PART // LANES), mirror).wait_recv()

            for row in range(rows_n):
                padded[row, LEFT : LEFT + cols_n, :] = (
                    tiles[slot, row, :, lanes].astype(jnp.float32) * mask
                )
            halves = range(cols_n // SUB)
            bias = jnp.broadcast_to(depth_bias[:, lanes].astype(jnp.float32), (SUB, LANES))
            sums = [[bias for _ in halves] for _ in range(rows_n)]
            for col in range(side):
                rows = [
                    [
                        padded[row, pl.ds(LEFT - reach + col + SUB * half, SUB), :]
                        for half in halves
                    ]
                    for row in range(rows_n)
                ]
                for row_off in range(side):
                    tap = taps[chunk, row_off * side + col]
                    for row in range(rows_n):
                        source = row + row_off - reach
                        if 0 <= source < rows_n:
                            for half in halves:
                                sums[row][half] = sums[row][half] + rows[source][half] * tap
            for row in range(rows_n):
                for half in halves:
                    spatial[row, SUB * half : SUB * (half + 1), lanes] = sums[row][half] * mask
            return carried

        lax.fori_loop(
            0, pieces_of(slot, channels, PART) * (PART // LANES), one_chunk, 0
        )
        inverse = 1.0 / jnp.full((1, 1), active, jnp.int32).astype(jnp.float32)
        gain = ln_gain[...].astype(jnp.float32)
        shift = ln_bias[...].astype(jnp.float32)

        def one_row(row, carried):
            value = spatial[row] * mask_all
            average = jnp.sum(value, axis=-1, keepdims=True) * inverse
            centred = (value - average) * mask_all
            variance = jnp.sum(centred * centred, axis=-1, keepdims=True) * inverse
            result = (centred * lax.rsqrt(variance + 1e-06) * gain + shift) * mask_all
            normed[slot, row * cols_n : (row + 1) * cols_n, :] = result.astype(
                jnp.bfloat16
            )
            return carried

        for row in range(rows_n):
            one_row(row, 0)

    def expand(slot, start, width):
        expanded = lax.dot_general(
            normed[slot],
            in_full[pl.ds(start, width), :],
            (((1,), (1,)), ((), ())),
            preferred_element_type=jnp.float32,
        )
        mask = (
            lax.broadcasted_iota(jnp.int32, (1, width), 1) + start < active_of(slot, hidden)
        ).astype(jnp.float32)
        return (jax.nn.gelu(expanded, approximate=True) * mask).astype(jnp.bfloat16)

    def add_to(slot, start):
        @pl.when(start < active_of(slot, hidden))
        def _():
            total[slot] += jnp.dot(
                expand(slot, start, 2 * piece),
                out_full[pl.ds(start, 2 * piece), :],
                preferred_element_type=jnp.float32,
            )

    def add_chip(other):
        start = pl.multiple_of(other * 2 * piece, 2 * piece)

        def one_slot(slot, carried):
            add_to(slot, start)
            return carried

        lax.fori_loop(0, count, one_slot, 0)

    width = 512 if hidden % 512 == 0 else hidden

    def activate(slot):
        def one_part(part, carried):
            start = pl.multiple_of(part * width, width)
            activated[:, pl.ds(start, width)] = expand(slot, start, width)
            return carried

        lax.fori_loop(0, pieces_of(slot, hidden, width), one_part, 0)

    def project(slot, part):
        lanes = pl.ds(pl.multiple_of(part * PART, PART), PART)

        def one_part(index, carried):
            start = pl.multiple_of(index * width, width)
            return carried + jnp.dot(
                activated[:, pl.ds(start, width)],
                out_full[pl.ds(start, width), lanes],
                preferred_element_type=jnp.float32,
            )

        total[slot, :, lanes] = lax.fori_loop(
            0,
            pieces_of(slot, hidden, width),
            one_part,
            jnp.zeros((rows_n * cols_n, PART), jnp.float32),
        )

    def finish(slot, part):
        start = pl.multiple_of(part * PART, PART)
        lanes = pl.ds(start, PART)
        mask = (
            lax.broadcasted_iota(jnp.int32, (1, PART), 1) + start < active_of(slot, channels)
        ).astype(jnp.float32)
        scale = layer_scale[:, lanes].astype(jnp.float32) * mask
        for row in range(rows_n):
            value = tiles[slot, row, :, lanes].astype(jnp.float32) * mask
            value = value + scale * total[slot, row * cols_n : (row + 1) * cols_n, lanes]
            results[slot, row, :, lanes] = value.astype(jnp.bfloat16)

    def forward(slot, part, target):
        lanes = pl.ds(pl.multiple_of(part * PART, PART), PART)
        return pltpu.make_async_remote_copy(
            src_ref=results.at[slot, :, :, lanes],
            dst_ref=tiles.at[slot, :, :, lanes],
            send_sem=tile_send.at[slot, part],
            recv_sem=tile_recv.at[slot, part],
            device_id={"section": target},
            device_id_type=MESH,
        )

    def across(slot, part):
        lanes = pl.ds(pl.multiple_of(part * PART, PART), PART)
        return pltpu.make_async_remote_copy(
            src_ref=results.at[slot, :, :, lanes],
            dst_ref=remote.at[slot, :, :, lanes],
            send_sem=store_send.at[slot, part],
            recv_sem=store_recv.at[slot, part],
            device_id={"section": mirror},
            device_id_type=MESH,
        )

    def each_part(slot, act):
        def one(part, carried):
            act(part)
            return carried

        lax.fori_loop(0, pieces_of(slot, channels, PART), one, 0)

    def norm_slot(slot, carried):
        total[slot] = jnp.zeros(total.shape[1:], jnp.float32)
        conv_norm(slot)
        return carried

    def siblings_in(other):
        for kind in range(2):
            weight_copy(kind, 2 * other + 1 - core, sibling, 0, 0).wait_recv()

    def absorb(step):
        rightward = chip - step
        leftward = chip + step

        @pl.when(rightward >= 0)
        def _():
            siblings_in(rightward)

            @pl.when(position == 0)
            def _():
                add_chip(rightward)

        @pl.when((leftward < chips) & (step > 0))
        def _():
            siblings_in(leftward)

            @pl.when(position == 0)
            def _():
                add_chip(leftward)

    def gather_step(step, carried):
        rightward = chip - step
        leftward = chip + step

        @pl.when((position == 0) & (step == 1))
        def _():
            lax.fori_loop(2, count, norm_slot, 0)

        @pl.when(step > 0)
        def _():
            absorb(step - 1)

        for kind in range(2):
            @pl.when(rightward >= 0)
            def _():
                shard = 2 * rightward + core

                @pl.when(step > 0)
                def _():
                    weight_copy(kind, shard, sibling, 0, step).wait_recv()

                @pl.when(chip + 1 < chips)
                def _():
                    weight_copy(kind, shard, rank + 2, 0, step).start()

            @pl.when(leftward < chips)
            def _():
                shard = 2 * leftward + core

                @pl.when(step > 0)
                def _():
                    weight_copy(kind, shard, sibling, 1, step).wait_recv()

                @pl.when(chip > 0)
                def _():
                    weight_copy(kind, shard, rank - 2, 1, step).start()

                @pl.when(step > 0)
                def _():
                    weight_copy(kind, shard, sibling, 3, step).start()

            @pl.when(rightward >= 0)
            def _():
                weight_copy(kind, 2 * rightward + core, sibling, 2, step).start()

        @pl.when((position == 0) & (step == 0))
        def _():
            lax.fori_loop(0, 2, norm_slot, 0)

        return carried

    lax.fori_loop(0, chips, gather_step, 0)
    at_end = (chip == 0) | (chip == chips - 1)
    far = chips - 1 - chip
    far_start = pl.multiple_of(far * 2 * piece, 2 * piece)

    @pl.when(at_end)
    def _():
        siblings_in(far)

    def one_slot(slot, carried):
        @pl.when(position > 0)
        def _():
            conv_norm(slot)
            activate(slot)

        @pl.when((position == 0) & at_end)
        def _():
            add_to(slot, far_start)

        def one_part(part):
            @pl.when(position > 0)
            def _():
                project(slot, part)

            finish(slot, part)

            @pl.when(position + 1 < sections)
            def _():
                forward(slot, part, position + 1).start()

        each_part(slot, one_part)

        @pl.when((slot != 1) & (position == sections - 1))
        def _():
            each_part(slot, lambda part: across(slot, part).start())

        return carried

    lax.fori_loop(0, count, one_slot, 0)
    sends_across = position != sections // 2 - 1
    takes_across = position != sections // 2

    def store_slot(slot, carried):
        @pl.when((slot != 1) & (position < sections - 1) & sends_across)
        def _():
            each_part(slot, lambda part: across(slot, part).start())

        def keep(part):
            lanes = pl.ds(pl.multiple_of(part * PART, PART), PART)
            for row in range(rows_n):
                remote[slot, row, :, lanes] = tiles[slot, row, :, lanes]

        @pl.when((slot != 1) & (position == sections // 2))
        def _():
            each_part(slot, keep)

        return carried

    lax.fori_loop(0, count, store_slot, 0)

    def drain_weights(step, carried):
        for kind in range(2):
            @pl.when(chip - step >= 0)
            def _():
                shard = 2 * (chip - step) + core

                @pl.when(chip + 1 < chips)
                def _():
                    weight_copy(kind, shard, rank + 2, 0, step).wait_send()

                weight_copy(kind, shard, sibling, 2, step).wait_send()

            @pl.when(chip + step < chips)
            def _():
                shard = 2 * (chip + step) + core

                @pl.when(chip > 0)
                def _():
                    weight_copy(kind, shard, rank - 2, 1, step).wait_send()

                @pl.when(step > 0)
                def _():
                    weight_copy(kind, shard, sibling, 3, step).wait_send()

        return carried

    lax.fori_loop(0, chips, drain_weights, 0)

    out[0] = results[jnp.where(full_low == 0, 1, jnp.where(half_low, 2, 3))]
    out[1] = results[jnp.where(full_low == 1, 1, jnp.where(half_low, 2, 3))]

    def drain_slot(slot, carried):
        @pl.when(position + 1 < sections)
        def _():
            each_part(slot, lambda part: forward(slot, part, mirror).wait_send())

        @pl.when((slot != 1) & sends_across)
        def _():
            each_part(slot, lambda part: across(slot, part).wait_send())

        @pl.when((slot != 1) & takes_across)
        def _():
            each_part(slot, lambda part: across(slot, part).wait_recv())

        return carried

    lax.fori_loop(0, count, drain_slot, 0)
    out[2] = remote[jnp.where(full_high == 2, 0, jnp.where(half_low, 3, 2))]
    out[3] = remote[jnp.where(full_high == 3, 0, jnp.where(half_low, 3, 2))]


def on_device(sections, shards, images, widths, *parameters):
    depth_kernel, depth_bias, ln_gain, ln_bias, w_in, w_out, layer_scale = parameters
    count, _, rows_n, cols_n, channels = images.shape
    side = depth_kernel.shape[1]
    hidden = w_in.shape[1] * shards
    tile = (count, rows_n, cols_n, channels)
    vmem = pl.BlockSpec(memory_space=pltpu.VMEM)
    anywhere = pl.BlockSpec(memory_space=pl.ANY)
    stored = pl.pallas_call(
        functools.partial(relay_kernel, sections, shards),
        out_shape=jax.ShapeDtypeStruct(tile, jnp.bfloat16),
        in_specs=[
            pl.BlockSpec(memory_space=pltpu.SMEM),
            anywhere,
            vmem,
            vmem,
            vmem,
            vmem,
            anywhere,
            anywhere,
            vmem,
        ],
        out_specs=vmem,
        scratch_shapes=[
            pltpu.VMEM((hidden, channels), jnp.bfloat16),
            pltpu.VMEM((hidden, channels), jnp.bfloat16),
            pltpu.VMEM(tile, jnp.bfloat16),
            pltpu.VMEM(tile, jnp.bfloat16),
            pltpu.VMEM(tile, jnp.bfloat16),
            pltpu.VMEM(tile, jnp.bfloat16),
            pltpu.VMEM((rows_n, cols_n + 2 * LEFT, LANES), jnp.float32),
            pltpu.VMEM((rows_n, cols_n, channels), jnp.float32),
            pltpu.VMEM((count, rows_n * cols_n, channels), jnp.bfloat16),
            pltpu.VMEM((count, rows_n * cols_n, channels), jnp.float32),
            pltpu.VMEM((rows_n * cols_n, hidden), jnp.bfloat16),
            pltpu.VMEM((channels // LANES, side * side, SUB, LANES), jnp.float32),
            pltpu.SemaphoreType.DMA((2,)),
            pltpu.SemaphoreType.DMA((count,)),
            pltpu.SemaphoreType.DMA((2, 4, shards // 2)),
            pltpu.SemaphoreType.DMA((2, shards)),
            pltpu.SemaphoreType.DMA((count, channels // PART)),
            pltpu.SemaphoreType.DMA((count, channels // PART)),
            pltpu.SemaphoreType.DMA((count, channels // PART)),
            pltpu.SemaphoreType.DMA((count, channels // PART)),
        ],
        compiler_params=pltpu.CompilerParams(collective_id=0, has_side_effects=True),
        name="relay",
    )(
        widths,
        images,
        depth_kernel,
        depth_bias,
        ln_gain,
        ln_bias,
        w_in,
        w_out,
        layer_scale,
    )
    return stored[None, :, None]


def solution(mesh):
    placed = (
        P(None, "dp", None, None, None),
        P(),
        P("section", None, None, None),
        P("section", None),
        P("section", None),
        P("section", None),
        P("section", "dp", None),
        P("section", "dp", None),
        P("section", None),
    )
    return jax.shard_map(
        functools.partial(on_device, mesh.shape["section"], mesh.shape["dp"]),
        mesh=mesh,
        in_specs=placed,
        out_specs=P("section", None, "dp", None, None, None),
        check_vma=False,
    )
```

```python
import functools

import jax
import jax.numpy as jnp
from jax import lax
from jax.experimental import pallas as pl
from jax.experimental.pallas import tpu as pltpu
from jax.sharding import PartitionSpec as P

MESH = pl.DeviceIdType.MESH
LANES = 128
LEFT = 8
PART = 256
SUB = 8


def active_of(slot, full):
    return jnp.where(slot < 2, full, jnp.where(slot == 2, full // 2, full // 4))


def pieces_of(slot, full, width):
    return (active_of(slot, full) + width - 1) // width


def relay_kernel(
    sections,
    shards,
    widths,
    images,
    depth_kernel,
    depth_bias,
    ln_gain,
    ln_bias,
    w_in,
    w_out,
    layer_scale,
    out,
    in_full,
    out_full,
    tiles,
    results,
    staged,
    remote,
    padded,
    spatial,
    normed,
    total,
    activated,
    taps,
    local_sem,
    tile_sem,
    weight_send,
    weight_recv,
    tile_send,
    tile_recv,
    store_send,
    store_recv,
):
    position = lax.axis_index("section")
    rank = lax.axis_index("dp")
    chips = shards // 2
    chip = rank // 2
    core = rank % 2
    sibling = rank + 1 - 2 * core
    mirror = sections - 1 - position
    count, rows_n, cols_n, channels = tiles.shape
    hidden = in_full.shape[0]
    piece = hidden // shards
    side = depth_kernel.shape[1]
    reach = side // 2
    full = (in_full, out_full)

    def span(shard):
        return pl.ds(pl.multiple_of(shard * piece, 16), piece)

    own = [
        pltpu.make_async_copy(source.at[0], full[kind].at[span(rank)], local_sem.at[kind])
        for kind, source in enumerate((w_in, w_out))
    ]
    for copy in own:
        copy.start()

    full_low = jnp.where(widths[0] == 0, 0, 1)
    full_high = jnp.where(widths[2] == 0, 2, 3)
    half_low = jnp.where(widths[0] == 0, widths[1], widths[0]) == 1
    small_low = 1 - full_low
    small_high = 5 - full_high
    order = (
        full_high,
        full_low,
        jnp.where(half_low, small_low, small_high),
        jnp.where(half_low, small_high, small_low),
    )

    def tile_in(slot):
        return pltpu.make_async_copy(images.at[slot, 0], staged.at[slot], tile_sem.at[slot])

    @pl.when(position == 0)
    def _():
        for slot in range(count):
            tile_in(slot).start()

    for slot in range(1, count):
        for row in range(rows_n):
            results[slot, row] = jnp.zeros((cols_n, channels), jnp.bfloat16)
            remote[slot, row] = jnp.zeros((cols_n, channels), jnp.bfloat16)

    barrier = pltpu.get_barrier_semaphore()
    pl.semaphore_signal(barrier, inc=1, device_id={"dp": sibling}, device_id_type=MESH)
    pl.semaphore_signal(barrier, inc=1, device_id={"section": mirror}, device_id_type=MESH)

    def greet(condition, target):
        @pl.when(condition)
        def _():
            pl.semaphore_signal(barrier, inc=1, device_id=target, device_id_type=MESH)

    greet(chip + 1 < chips, {"dp": rank + 2})
    greet(chip > 0, {"dp": rank - 2})
    greet(position + 1 < sections, {"section": position + 1})
    greet(position > 0, {"section": position - 1})

    for row in range(rows_n):
        padded[row, 0:LEFT, :] = jnp.zeros((LEFT, LANES), jnp.float32)
        padded[row, LEFT + cols_n :, :] = jnp.zeros((LEFT, LANES), jnp.float32)

    def spread(chunk, carried):
        lanes = pl.ds(pl.multiple_of(chunk * LANES, LANES), LANES)
        for row in range(side):
            strip = depth_kernel[0, row, :, lanes].astype(jnp.float32)
            for col in range(side):
                taps[chunk, row * side + col] = jnp.broadcast_to(
                    strip[col : col + 1, :], (SUB, LANES)
                )
        return carried

    lax.fori_loop(0, channels // LANES, spread, 0)
    for copy in own:
        copy.wait()

    greeted = 2 + sum(
        jnp.where(condition, 1, 0)
        for condition in (
            chip + 1 < chips,
            chip > 0,
            position + 1 < sections,
            position > 0,
        )
    )
    pl.semaphore_wait(barrier, greeted)

    @pl.when(position == 0)
    def _():
        for slot in range(count):
            tile_in(slot).wait()
        for slot in range(count):
            tiles[slot] = staged[order[slot]]

    def weight_copy(kind, shard, target, lane, step):
        return pltpu.make_async_remote_copy(
            src_ref=full[kind].at[span(shard)],
            dst_ref=full[kind].at[span(shard)],
            send_sem=weight_send.at[kind, lane, step],
            recv_sem=weight_recv.at[kind, shard],
            device_id={"dp": target},
            device_id_type=MESH,
        )

    def conv_norm(slot):
        active = active_of(slot, channels)
        mask_all = (lax.broadcasted_iota(jnp.int32, (1, channels), 1) < active).astype(jnp.float32)

        def one_chunk(chunk, carried):
            start = pl.multiple_of(chunk * LANES, LANES)
            lanes = pl.ds(start, LANES)
            mask = (lax.broadcasted_iota(jnp.int32, (1, LANES), 1) + start < active).astype(
                jnp.float32
            )

            @pl.when((position > 0) & (chunk % (PART // LANES) == 0))
            def _():
                forward(slot, chunk // (PART // LANES), mirror).wait_recv()

            for row in range(rows_n):
                padded[row, LEFT : LEFT + cols_n, :] = (
                    tiles[slot, row, :, lanes].astype(jnp.float32) * mask
                )
            halves = range(cols_n // SUB)
            bias = jnp.broadcast_to(depth_bias[:, lanes].astype(jnp.float32), (SUB, LANES))
            sums = [[bias for _ in halves] for _ in range(rows_n)]
            for col in range(side):
                rows = [
                    [
                        padded[row, pl.ds(LEFT - reach + col + SUB * half, SUB), :]
                        for half in halves
                    ]
                    for row in range(rows_n)
                ]
                for row_off in range(side):
                    tap = taps[chunk, row_off * side + col]
                    for row in range(rows_n):
                        source = row + row_off - reach
                        if 0 <= source < rows_n:
                            for half in halves:
                                sums[row][half] = sums[row][half] + rows[source][half] * tap
            for row in range(rows_n):
                for half in halves:
                    spatial[row, SUB * half : SUB * (half + 1), lanes] = sums[row][half] * mask
            return carried

        lax.fori_loop(
            0, pieces_of(slot, channels, PART) * (PART // LANES), one_chunk, 0
        )
        inverse = 1.0 / jnp.full((1, 1), active, jnp.int32).astype(jnp.float32)
        gain = ln_gain[...].astype(jnp.float32)
        shift = ln_bias[...].astype(jnp.float32)

        def one_row(row, carried):
            value = spatial[row] * mask_all
            average = jnp.sum(value, axis=-1, keepdims=True) * inverse
            centred = (value - average) * mask_all
            variance = jnp.sum(centred * centred, axis=-1, keepdims=True) * inverse
            result = (centred * lax.rsqrt(variance + 1e-06) * gain + shift) * mask_all
            normed[slot, row * cols_n : (row + 1) * cols_n, :] = result.astype(
                jnp.bfloat16
            )
            return carried

        for row in range(rows_n):
            one_row(row, 0)

    def expand(slot, start, width):
        expanded = lax.dot_general(
            normed[slot],
            in_full[pl.ds(start, width), :],
            (((1,), (1,)), ((), ())),
            preferred_element_type=jnp.float32,
        )
        mask = (
            lax.broadcasted_iota(jnp.int32, (1, width), 1) + start < active_of(slot, hidden)
        ).astype(jnp.float32)
        return (jax.nn.gelu(expanded, approximate=True) * mask).astype(jnp.bfloat16)

    def add_to(slot, start):
        @pl.when(start < active_of(slot, hidden))
        def _():
            total[slot] += jnp.dot(
                expand(slot, start, 2 * piece),
                out_full[pl.ds(start, 2 * piece), :],
                preferred_element_type=jnp.float32,
            )

    def add_chip(other):
        start = pl.multiple_of(other * 2 * piece, 2 * piece)

        def one_slot(slot, carried):
            add_to(slot, start)
            return carried

        lax.fori_loop(0, count, one_slot, 0)

    width = 512 if hidden % 512 == 0 else hidden

    def activate(slot):
        def one_part(part, carried):
            start = pl.multiple_of(part * width, width)
            activated[:, pl.ds(start, width)] = expand(slot, start, width)
            return carried

        lax.fori_loop(0, pieces_of(slot, hidden, width), one_part, 0)

    def project(slot, part):
        lanes = pl.ds(pl.multiple_of(part * PART, PART), PART)

        def one_part(index, carried):
            start = pl.multiple_of(index * width, width)
            return carried + jnp.dot(
                activated[:, pl.ds(start, width)],
                out_full[pl.ds(start, width), lanes],
                preferred_element_type=jnp.float32,
            )

        total[slot, :, lanes] = lax.fori_loop(
            0,
            pieces_of(slot, hidden, width),
            one_part,
            jnp.zeros((rows_n * cols_n, PART), jnp.float32),
        )

    def finish(slot, part):
        start = pl.multiple_of(part * PART, PART)
        lanes = pl.ds(start, PART)
        mask = (
            lax.broadcasted_iota(jnp.int32, (1, PART), 1) + start < active_of(slot, channels)
        ).astype(jnp.float32)
        scale = layer_scale[:, lanes].astype(jnp.float32) * mask
        for row in range(rows_n):
            value = tiles[slot, row, :, lanes].astype(jnp.float32) * mask
            value = value + scale * total[slot, row * cols_n : (row + 1) * cols_n, lanes]
            results[slot, row, :, lanes] = value.astype(jnp.bfloat16)

    def forward(slot, part, target):
        lanes = pl.ds(pl.multiple_of(part * PART, PART), PART)
        return pltpu.make_async_remote_copy(
            src_ref=results.at[slot, :, :, lanes],
            dst_ref=tiles.at[slot, :, :, lanes],
            send_sem=tile_send.at[slot, part],
            recv_sem=tile_recv.at[slot, part],
            device_id={"section": target},
            device_id_type=MESH,
        )

    def across(slot, part):
        lanes = pl.ds(pl.multiple_of(part * PART, PART), PART)
        return pltpu.make_async_remote_copy(
            src_ref=results.at[slot, :, :, lanes],
            dst_ref=remote.at[slot, :, :, lanes],
            send_sem=store_send.at[slot, part],
            recv_sem=store_recv.at[slot, part],
            device_id={"section": mirror},
            device_id_type=MESH,
        )

    def each_part(slot, act):
        def one(part, carried):
            act(part)
            return carried

        lax.fori_loop(0, pieces_of(slot, channels, PART), one, 0)

    def norm_slot(slot, carried):
        total[slot] = jnp.zeros(total.shape[1:], jnp.float32)
        conv_norm(slot)
        return carried

    def siblings_in(other):
        for kind in range(2):
            weight_copy(kind, 2 * other + 1 - core, sibling, 0, 0).wait_recv()

    def absorb(step):
        rightward = chip - step
        leftward = chip + step

        @pl.when(rightward >= 0)
        def _():
            siblings_in(rightward)

            @pl.when(position == 0)
            def _():
                add_chip(rightward)

        @pl.when((leftward < chips) & (step > 0))
        def _():
            siblings_in(leftward)

            @pl.when(position == 0)
            def _():
                add_chip(leftward)

    def gather_step(step, carried):
        rightward = chip - step
        leftward = chip + step

        @pl.when((position == 0) & (step == 1))
        def _():
            lax.fori_loop(2, count, norm_slot, 0)

        @pl.when(step > 0)
        def _():
            absorb(step - 1)

        for kind in range(2):
            @pl.when(rightward >= 0)
            def _():
                shard = 2 * rightward + core

                @pl.when(step > 0)
                def _():
                    weight_copy(kind, shard, sibling, 0, step).wait_recv()

                @pl.when(chip + 1 < chips)
                def _():
                    weight_copy(kind, shard, rank + 2, 0, step).start()

            @pl.when(leftward < chips)
            def _():
                shard = 2 * leftward + core

                @pl.when(step > 0)
                def _():
                    weight_copy(kind, shard, sibling, 1, step).wait_recv()

                @pl.when(chip > 0)
                def _():
                    weight_copy(kind, shard, rank - 2, 1, step).start()

                @pl.when(step > 0)
                def _():
                    weight_copy(kind, shard, sibling, 3, step).start()

            @pl.when(rightward >= 0)
            def _():
                weight_copy(kind, 2 * rightward + core, sibling, 2, step).start()

        @pl.when((position == 0) & (step == 0))
        def _():
            lax.fori_loop(0, 2, norm_slot, 0)

        return carried

    lax.fori_loop(0, chips, gather_step, 0)
    at_end = (chip == 0) | (chip == chips - 1)
    far = chips - 1 - chip
    far_start = pl.multiple_of(far * 2 * piece, 2 * piece)

    @pl.when(at_end)
    def _():
        siblings_in(far)

    inner = (position > 0) & (position < sections - 1)
    sends_across = position != sections // 2 - 1
    takes_across = position != sections // 2

    def one_slot(slot, carried):
        @pl.when(position > 0)
        def _():
            conv_norm(slot)
            activate(slot)

        @pl.when((position == 0) & at_end)
        def _():
            add_to(slot, far_start)

        def one_part(part):
            @pl.when(position > 0)
            def _():
                project(slot, part)

            finish(slot, part)

            @pl.when(position + 1 < sections)
            def _():
                forward(slot, part, position + 1).start()

        each_part(slot, one_part)

        @pl.when((slot != 1) & (position == sections - 1))
        def _():
            each_part(slot, lambda part: across(slot, part).start())

        @pl.when((slot == 2) & inner & sends_across)
        def _():
            each_part(0, lambda part: across(0, part).start())

        return carried

    lax.fori_loop(0, count, one_slot, 0)

    def store_slot(slot, carried):
        early = (slot == 0) & inner

        @pl.when((slot != 1) & (position < sections - 1) & sends_across & ~early)
        def _():
            each_part(slot, lambda part: across(slot, part).start())

        def keep(part):
            lanes = pl.ds(pl.multiple_of(part * PART, PART), PART)
            for row in range(rows_n):
                remote[slot, row, :, lanes] = tiles[slot, row, :, lanes]

        @pl.when((slot != 1) & (position == sections // 2))
        def _():
            each_part(slot, keep)

        return carried

    lax.fori_loop(0, count, store_slot, 0)

    def drain_weights(step, carried):
        for kind in range(2):
            @pl.when(chip - step >= 0)
            def _():
                shard = 2 * (chip - step) + core

                @pl.when(chip + 1 < chips)
                def _():
                    weight_copy(kind, shard, rank + 2, 0, step).wait_send()

                weight_copy(kind, shard, sibling, 2, step).wait_send()

            @pl.when(chip + step < chips)
            def _():
                shard = 2 * (chip + step) + core

                @pl.when(chip > 0)
                def _():
                    weight_copy(kind, shard, rank - 2, 1, step).wait_send()

                @pl.when(step > 0)
                def _():
                    weight_copy(kind, shard, sibling, 3, step).wait_send()

        return carried

    lax.fori_loop(0, chips, drain_weights, 0)

    out[0] = results[jnp.where(full_low == 0, 1, jnp.where(half_low, 2, 3))]
    out[1] = results[jnp.where(full_low == 1, 1, jnp.where(half_low, 2, 3))]

    def drain_slot(slot, carried):
        @pl.when(position + 1 < sections)
        def _():
            each_part(slot, lambda part: forward(slot, part, mirror).wait_send())

        @pl.when((slot != 1) & sends_across)
        def _():
            each_part(slot, lambda part: across(slot, part).wait_send())

        @pl.when((slot != 1) & takes_across)
        def _():
            each_part(slot, lambda part: across(slot, part).wait_recv())

        return carried

    lax.fori_loop(0, count, drain_slot, 0)
    out[2] = remote[jnp.where(full_high == 2, 0, jnp.where(half_low, 3, 2))]
    out[3] = remote[jnp.where(full_high == 3, 0, jnp.where(half_low, 3, 2))]


def on_device(sections, shards, images, widths, *parameters):
    depth_kernel, depth_bias, ln_gain, ln_bias, w_in, w_out, layer_scale = parameters
    count, _, rows_n, cols_n, channels = images.shape
    side = depth_kernel.shape[1]
    hidden = w_in.shape[1] * shards
    tile = (count, rows_n, cols_n, channels)
    vmem = pl.BlockSpec(memory_space=pltpu.VMEM)
    anywhere = pl.BlockSpec(memory_space=pl.ANY)
    stored = pl.pallas_call(
        functools.partial(relay_kernel, sections, shards),
        out_shape=jax.ShapeDtypeStruct(tile, jnp.bfloat16),
        in_specs=[
            pl.BlockSpec(memory_space=pltpu.SMEM),
            anywhere,
            vmem,
            vmem,
            vmem,
            vmem,
            anywhere,
            anywhere,
            vmem,
        ],
        out_specs=vmem,
        scratch_shapes=[
            pltpu.VMEM((hidden, channels), jnp.bfloat16),
            pltpu.VMEM((hidden, channels), jnp.bfloat16),
            pltpu.VMEM(tile, jnp.bfloat16),
            pltpu.VMEM(tile, jnp.bfloat16),
            pltpu.VMEM(tile, jnp.bfloat16),
            pltpu.VMEM(tile, jnp.bfloat16),
            pltpu.VMEM((rows_n, cols_n + 2 * LEFT, LANES), jnp.float32),
            pltpu.VMEM((rows_n, cols_n, channels), jnp.float32),
            pltpu.VMEM((count, rows_n * cols_n, channels), jnp.bfloat16),
            pltpu.VMEM((count, rows_n * cols_n, channels), jnp.float32),
            pltpu.VMEM((rows_n * cols_n, hidden), jnp.bfloat16),
            pltpu.VMEM((channels // LANES, side * side, SUB, LANES), jnp.float32),
            pltpu.SemaphoreType.DMA((2,)),
            pltpu.SemaphoreType.DMA((count,)),
            pltpu.SemaphoreType.DMA((2, 4, shards // 2)),
            pltpu.SemaphoreType.DMA((2, shards)),
            pltpu.SemaphoreType.DMA((count, channels // PART)),
            pltpu.SemaphoreType.DMA((count, channels // PART)),
            pltpu.SemaphoreType.DMA((count, channels // PART)),
            pltpu.SemaphoreType.DMA((count, channels // PART)),
        ],
        compiler_params=pltpu.CompilerParams(collective_id=0, has_side_effects=True),
        name="relay",
    )(
        widths,
        images,
        depth_kernel,
        depth_bias,
        ln_gain,
        ln_bias,
        w_in,
        w_out,
        layer_scale,
    )
    return stored[None, :, None]


def solution(mesh):
    placed = (
        P(None, "dp", None, None, None),
        P(),
        P("section", None, None, None),
        P("section", None),
        P("section", None),
        P("section", None),
        P("section", "dp", None),
        P("section", "dp", None),
        P("section", None),
    )
    return jax.shard_map(
        functools.partial(on_device, mesh.shape["section"], mesh.shape["dp"]),
        mesh=mesh,
        in_specs=placed,
        out_specs=P("section", None, "dp", None, None, None),
        check_vma=False,
    )
```
